32 devices in a mesh: row: 16 (over z, y, core), col: 2 (over x).
Axes of the slice: x: 2, y: 2, z: 4, core: 2. Of those that a mesh axis runs over, the one named last changes fastest.
Arguments:
- features: bfloat16 [12, 64, 64, 128], P(None, 'row', 'col'), may hold values from -6 to 6
- cotangent: bfloat16 [12, 32, 32, 128], P(None, 'row', 'col'), may hold values from -0.25 to 0.25
- conv_weight: bfloat16 [1152, 512], P('row', 'col'), may hold values from -0.1875 to 0.1875
- projection_weight: bfloat16 [512, 128], P('row', 'col'), may hold values from -0.25 to 0.25
- down_weight: bfloat16 [512, 128], P('row', 'col'), may hold values from -0.25 to 0.25
- edge_links: int32 [12, 4, 3], replicated, may hold values from 0 to 11, as said below
- corner_links: int32 [12, 4, 3], replicated, may hold values from -1 to 11, as said below
Outputs:
- block_out: bfloat16 [12, 32, 32, 128], P(None, 'row', 'col')
- grad_conv: float32 [1152, 512], P('row', 'col')
- projection_gradient: float32 [512, 128], P('row', 'col')
- grad_down: float32 [512, 128], P('row', 'col')
The draws below stay inside these ranges and needn't reach their ends.
Inputs may be any that keep to these rules, and one draw needn't show every extreme that they name: edge_links[f, s] = (g, t, r): the halo beyond side s of face f is read from side t of face g, positions reversed when r = 1; pairs are mutual and g differs from f; the links are those of the HEALPix sphere with the faces relabelled and each face turned by a multiple of 90 degrees. corner_links[f, e] = (g, e', w): the diagonal face across corner e of face f, its corner, and a swap flag; g = -1 (and e' = w = 0) at the corners where only three faces meet, which are two corners of every face.
All inputs are finite; a program needn't handle non-finite values.
Results may differ from the reference program's by a relative error of at most 0.0052.
Values may be sent and summed in bfloat16 or wider, within the bound.
No kernel may reach another device: no remote copies, remote signals or barrier semaphores. Data moves between devices by JAX's collectives and lax.ppermute only.
A program may use at most 64 MiB of HBM per device.

```python
import jax
import jax.numpy as jnp
import numpy as np
from jax import lax

C = 128
HID = 512
DILATION_STEP = 2
FACES = 12
FS = 64
HALF = 32


def canonical_links():
    side_face = np.zeros((12, 4), np.int32)
    side_side = np.zeros((12, 4), np.int32)
    corner_face = -np.ones((12, 4), np.int32)
    corner_corner = np.zeros((12, 4), np.int32)
    for index in range(4):
        after = (index + 1) % 4
        before = (index + 3) % 4
        across = (index + 2) % 4
        side_face[index] = [after, 4 + after, 4 + index, before]
        side_side[index] = [3, 3, 0, 0]
        side_face[4 + index] = [index, 8 + index, 8 + before, before]
        side_side[4 + index] = [2, 3, 0, 1]
        side_face[8 + index] = [4 + after, 8 + after, 8 + before, 4 + index]
        side_side[8 + index] = [2, 2, 1, 1]
        corner_face[index, 0] = across
        corner_corner[index, 0] = 0
        corner_face[index, 2] = 8 + index
        corner_corner[index, 2] = 0
        corner_face[4 + index, 1] = 4 + after
        corner_corner[4 + index, 1] = 3
        corner_face[4 + index, 3] = 4 + before
        corner_corner[4 + index, 3] = 1
        corner_face[8 + index, 0] = index
        corner_corner[8 + index, 0] = 2
        corner_face[8 + index, 2] = 8 + across
        corner_corner[8 + index, 2] = 2
    return (side_face, side_side, corner_face, corner_corner)


def reversal(side, turn):
    counter = jnp.arange(4, dtype=jnp.int32)
    passes = (side[..., None] + counter) % 2 * (counter < turn[..., None]).astype(jnp.int32)
    return jnp.sum(passes, axis=-1) % 2


def linked_tables(key):
    key = jax.random.fold_in(key, 11)
    perm_key, turn_key = jax.random.split(key)
    order = jax.random.permutation(perm_key, 12).astype(jnp.int32)
    turns = jax.random.randint(turn_key, (12,), 0, 4).astype(jnp.int32)
    side_face, side_side, corner_face, corner_corner = canonical_links()
    side_face = jnp.asarray(side_face)
    side_side = jnp.asarray(side_side)
    corner_face = jnp.asarray(corner_face)
    corner_corner = jnp.asarray(corner_corner)
    sides = jnp.broadcast_to(jnp.arange(4, dtype=jnp.int32)[None, :], (12, 4))
    own_turn = jnp.broadcast_to(turns[:, None], (12, 4))
    stored_side = (sides + own_turn) % 4
    own_rev = reversal(sides, own_turn)
    other_turn = turns[side_face]
    other_side = (side_side + other_turn) % 4
    other_rev = reversal(side_side, other_turn)
    flip = (own_rev + other_rev) % 2
    face_rows = jnp.broadcast_to(order[:, None], (12, 4))
    edge_values = jnp.stack([order[side_face], other_side, flip], axis=-1).astype(jnp.int32)
    edge_table = jnp.zeros((12, 4, 3), jnp.int32).at[face_rows, stored_side].set(edge_values)
    present = corner_face >= 0
    safe_face = jnp.maximum(corner_face, 0)
    other_corner = (corner_corner + turns[safe_face]) % 4
    swap_flag = (own_turn + turns[safe_face]) % 2
    corner_entries = jnp.stack([jnp.where(present, order[safe_face], -1), jnp.where(present, other_corner, 0), jnp.where(present, swap_flag, 0)], axis=-1).astype(jnp.int32)
    corner_table = jnp.zeros((12, 4, 3), jnp.int32).at[face_rows, stored_side].set(corner_entries)
    return (edge_table, corner_table)


def draw_edge_links(key, part):
    return linked_tables(key)[0]


def draw_corner_links(key, part):
    return linked_tables(key)[1]


def shard_levels(rng, shape, shards, low, top_value):
    def one(dim, blocks):
        heights = jax.random.uniform(jax.random.fold_in(jax.random.fold_in(rng, 6), dim), (blocks,), jnp.float32, low / len(shards), top_value / len(shards))
        return jnp.repeat(jnp.exp(heights), shape[dim] // blocks).reshape((-1,) + (1,) * (len(shape) - dim - 1))

    factor_of = one(*shards[0])
    for cut in shards[1:]:
        factor_of = factor_of * one(*cut)
    return factor_of


def scatter_about(stream_key, dims, width, limit, pieces=(), kind=jnp.bfloat16):
    entries = jax.random.normal(stream_key, dims, jnp.float32) * width
    if len(pieces) > 0:
        entries = shard_levels(stream_key, dims, pieces, -0.22, 0.18) * entries
    return jnp.clip(entries, min=-limit, max=limit).astype(kind)


def setup_inputs(seed: int = 0) -> dict:
    keys = jax.random.split(jax.random.key(seed), 8)
    features = scatter_about(keys[0], (FACES, FS, FS, C), 1.0, 6.0, ((1, 16), (2, 2)))
    cotangent = scatter_about(keys[1], (FACES, HALF, HALF, C), (1.0 / FS), 0.25, ((1, 16), (2, 2)))
    conv_weight = scatter_about(keys[2], (9 * C, HID), (9 * C) ** -0.5, 0.1875, ((0, 16), (1, 2)))
    projection_weight = scatter_about(keys[3], (HID, C), HID ** -0.5, 0.25, ((0, 16), (1, 2)))
    down_weight = scatter_about(keys[4], (4 * C, C), (4 * C) ** -0.5, 0.25, ((0, 16), (1, 2)))
    edge_links = draw_edge_links(jax.random.fold_in(keys[7], 71), 0)
    corner_links = draw_corner_links(jax.random.fold_in(keys[7], 71), 0)
    return dict(features=features, cotangent=cotangent, conv_weight=conv_weight, projection_weight=projection_weight, down_weight=down_weight, edge_links=edge_links, corner_links=corner_links)


def gelu_value(values):
    return 0.5 * values * (1.0 + jax.scipy.special.erf(values * 0.7071067811865476))


def gelu_slope(values):
    erf_part = 0.5 * (1.0 + jax.scipy.special.erf(values * 0.7071067811865476))
    return erf_part + values * jnp.exp(-0.5 * values * values) * 0.3989422804014327


def side_strips(top_side, right_side, bottom_side, left_side):
    return jnp.stack([top_side, jnp.swapaxes(right_side, 1, 2)[:, ::-1], bottom_side[:, ::-1], jnp.swapaxes(left_side, 1, 2)])


def corner_blocks(top_side, bottom_side, channel_depth):
    extent = top_side.shape[2]
    upper_left = top_side[:, :, :channel_depth]
    upper_right = top_side[:, :, extent - channel_depth:][:, :, ::-1]
    lower_right = bottom_side[:, ::-1, extent - channel_depth:][:, :, ::-1]
    bottom_left_corner = bottom_side[:, ::-1, :channel_depth]
    return jnp.stack([upper_left, upper_right, lower_right, bottom_left_corner])


def border_bands(top_side, right_side, bottom_side, left_side, edge_links, corner_links):
    channel_depth = top_side.shape[1]
    strips = side_strips(top_side, right_side, bottom_side, left_side)
    blocks = corner_blocks(top_side, bottom_side, channel_depth)
    picked = strips[edge_links[:, :, 1], edge_links[:, :, 0]]
    flipped = edge_links[:, :, 2][:, :, None, None, None] == 1
    picked = jnp.where(flipped, picked[:, :, :, ::-1], picked)
    present = corner_links[:, :, 0]
    patches = blocks[corner_links[:, :, 1], jnp.maximum(present, 0)]
    swapped = corner_links[:, :, 2][:, :, None, None, None] == 1
    patches = jnp.where(swapped, jnp.swapaxes(patches, 2, 3), patches)
    patches = jnp.where(present[:, :, None, None, None] >= 0, patches, jnp.zeros_like(patches))
    top_band = jnp.concatenate([patches[:, 0, ::-1, ::-1], picked[:, 0, ::-1], patches[:, 1, ::-1, :]], axis=2)
    bottom_band = jnp.concatenate([patches[:, 3, :, ::-1], picked[:, 2], patches[:, 2]], axis=2)
    left_band = jnp.swapaxes(picked[:, 3, ::-1], 1, 2)
    right_band = jnp.swapaxes(picked[:, 1], 1, 2)
    return top_band, bottom_band, left_band, right_band


def face_pass(totals, items, conv_full, proj_full, down_full):
    padded_face, face_values, face_cotangent = items
    height, breadth, channels = face_values.shape
    channel_depth = (padded_face.shape[0] - height) // 2
    hidden_width = conv_full.shape[1]
    pixels = height * breadth
    windows = []
    pre_act = jnp.zeros((pixels, hidden_width), jnp.float32)
    for row_tap in range(3):
        for col_tap in range(3):
            window = padded_face[row_tap * channel_depth: row_tap * channel_depth + height, col_tap * channel_depth: col_tap * channel_depth + breadth]
            window = window.reshape(pixels, channels)
            windows.append(window)
            offset = (3 * row_tap + col_tap) * channels
            pre_act = pre_act + jnp.dot(window, conv_full[offset: offset + channels], preferred_element_type=jnp.float32)
    hidden = gelu_value(pre_act).astype(jnp.bfloat16)
    resid = (face_values.reshape(pixels, channels).astype(jnp.float32) + jnp.dot(hidden, proj_full, preferred_element_type=jnp.float32)).astype(jnp.bfloat16)
    grouped = resid.reshape(height // 2, 2, breadth // 2, 2, channels).transpose(0, 2, 1, 3, 4).reshape(pixels // 4, 4 * channels)
    block_out = jnp.dot(grouped, down_full, preferred_element_type=jnp.float32).astype(jnp.bfloat16)
    block_out = block_out.reshape(height // 2, breadth // 2, channels)
    upstream = face_cotangent.reshape(pixels // 4, channels)
    grad_down = jnp.dot(grouped.T, upstream, preferred_element_type=jnp.float32)
    gresid = jnp.dot(upstream, down_full.T, preferred_element_type=jnp.float32).astype(jnp.bfloat16)
    gresid = gresid.reshape(height // 2, breadth // 2, 2, 2, channels).transpose(0, 2, 1, 3, 4).reshape(pixels, channels)
    projection_gradient = jnp.dot(hidden.T, gresid, preferred_element_type=jnp.float32)
    gpre = (jnp.dot(gresid, proj_full.T, preferred_element_type=jnp.float32) * gelu_slope(pre_act)).astype(jnp.bfloat16)
    grad_conv = jnp.concatenate([jnp.dot(window.T, gpre, preferred_element_type=jnp.float32) for window in windows], axis=0)
    totals = (totals[0] + grad_conv, totals[1] + projection_gradient, totals[2] + grad_down)
    return totals, block_out


def reference(features, cotangent, conv_weight, projection_weight, down_weight, edge_links, corner_links):
    channel_depth = DILATION_STEP
    extent = FS
    top_side = features[:, :channel_depth]
    right_side = features[:, :, extent - channel_depth:]
    bottom_side = features[:, extent - channel_depth:]
    left_side = features[:, :, :channel_depth]
    top_band, bottom_band, left_band, right_band = border_bands(top_side, right_side, bottom_side, left_side, edge_links, corner_links)
    middle = jnp.concatenate([left_band, features, right_band], axis=2)
    padded = jnp.concatenate([top_band, middle, bottom_band], axis=1)
    start = (jnp.zeros(conv_weight.shape, jnp.float32), jnp.zeros(projection_weight.shape, jnp.float32), jnp.zeros(down_weight.shape, jnp.float32))

    def one_face(totals, items):
        return face_pass(totals, items, conv_weight, projection_weight, down_weight)

    totals, block_out = lax.scan(one_face, start, (padded, features, cotangent))
    return block_out, totals[0], totals[1], totals[2]
```

```python
import functools

import jax
import jax.numpy as jnp
from jax import lax
from jax.experimental import pallas as pl
from jax.experimental.pallas import tpu as pltpu
from jax.sharding import PartitionSpec as P

DEPTH = 2
BF = jnp.bfloat16
F32 = jnp.float32


def swap(value, axis, bit):
    count = lax.axis_size(axis)
    return lax.ppermute(value, axis, [(i, i ^ bit) for i in range(count)])


def gather_pair(value, axis, dim):
    if lax.axis_size(axis) != 2:
        return lax.all_gather(value, axis, axis=dim, tiled=True)
    other = swap(value, axis, 1)
    first = lax.axis_index(axis) == 0
    low = jnp.where(first, value, other)
    high = jnp.where(first, other, value)
    return jnp.concatenate([low, high], axis=dim)


def scatter_sum_pair(value, axis, dim):
    count = lax.axis_size(axis)
    if count != 2:
        return lax.psum_scatter(value, axis, scatter_dimension=dim, tiled=True)
    low, high = jnp.split(value, 2, axis=dim)
    first = lax.axis_index(axis) == 0
    return jnp.where(first, low, high) + swap(jnp.where(first, high, low), axis, 1)


def pack_cols(value):
    width = value.shape[-1]
    if width % 128 == 0:
        return jnp.concatenate(
            [value[..., j : j + 128] for j in range(0, width, 128)], axis=-2
        )
    return value.reshape(value.shape[:-2] + (-1, 128))


def unpack_cols(value, width):
    if width % 128 == 0:
        parts = width // 128
        rows = value.shape[-2] // parts
        return jnp.concatenate(
            [value[..., j * rows : (j + 1) * rows, :] for j in range(parts)], axis=-1
        )
    return value.reshape(value.shape[:-2] + (-1, width))


def dot(a, b, dims=((1,), (0,))):
    return lax.dot_general(a, b, (dims, ((), ())), preferred_element_type=F32)


def block_kernel(
    group, last_row, edge, corner, where_ref,
    feat, up, down_rows, near, own, far, sides, cot, wc, pj, dw,
    out_ref, gc_ref, pg_ref, gd_ref,
    pad, shifted, resid_scr,
):
    step = pl.program_id(0)
    row = where_ref[0]
    col = where_ref[1]
    height, width = feat.shape[1], feat.shape[2]
    tall = height + 2 * DEPTH
    base = 8

    @pl.when(step == 0)
    def _():
        gc_ref[...] = jnp.zeros_like(gc_ref)
        pg_ref[...] = jnp.zeros_like(pg_ref)
        gd_ref[...] = jnp.zeros_like(gd_ref)

    line = lax.broadcasted_iota(jnp.int32, (width, width), 0)
    across = lax.broadcasted_iota(jnp.int32, (width, width), 1)
    flip = (line + across == width - 1).astype(BF)

    for j in range(group):
        face = step * group + j
        pad[DEPTH : DEPTH + height, base : base + width, :] = feat[j].astype(F32)
        pad[:DEPTH, base : base + width, :] = up[j].astype(F32)
        pad[DEPTH + height :, base : base + width, :] = down_rows[j].astype(F32)

        def link(side, what):
            return edge[face * 12 + side * 3 + what]

        for side, column in ((3, lambda k: base - 1 - k), (1, lambda k: base + width + k)):
            g, t, rev = link(side, 0), link(side, 1), link(side, 2)
            for k in range(DEPTH):
                for i in range(tall):
                    pick = jnp.where(rev == 1, tall - 1 - i, i)
                    pad[i, column(k) : column(k) + 1, :] = near[rev, t, g, k, pl.ds(pick, 1), :]

        def frame(side, corners, line_of, mine):
            g, t, rev = link(side, 0), link(side, 1), link(side, 2)
            for k in range(DEPTH):
                picked = jnp.where(
                    t == mine, own[g, k].astype(F32),
                    jnp.where(t == 2 - mine, far[g, k].astype(F32), sides[face, k].astype(F32)),
                ).astype(BF)
                turned = dot(flip, picked)
                pad[line_of(k), base : base + width, :] = jnp.where(
                    rev == 1, turned, picked.astype(F32)
                )
            for e, column in corners:
                cg = corner[face * 12 + e * 3]
                ce = corner[face * 12 + e * 3 + 1]
                cw = corner[face * 12 + e * 3 + 2]
                upper = ce < 2
                t = jnp.where((ce == 0) | (ce == 3), 3, 1)
                away = jnp.where(upper == (mine == 0), 0, 1)
                for a in range(DEPTH):
                    for b in range(DEPTH):
                        u = jnp.where(cw == 1, b, a)
                        v = jnp.where(cw == 1, a, b)
                        i = jnp.where(upper, DEPTH + u, tall - 1 - DEPTH - u)
                        value = near[away, t, jnp.maximum(cg, 0), v, pl.ds(i, 1), :]
                        pad[line_of(a), column(b) : column(b) + 1, :] = jnp.where(
                            cg >= 0, value, jnp.zeros_like(value)
                        )

        @pl.when(row == 0)
        def _():
            frame(
                0,
                ((0, lambda b: base - 1 - b), (1, lambda b: base + width + b)),
                lambda k: DEPTH - 1 - k,
                0,
            )

        @pl.when(row == last_row)
        def _():
            frame(
                2,
                ((3, lambda b: base - 1 - b), (2, lambda b: base + width + b)),
                lambda k: DEPTH + height + k,
                2,
            )

        for tap in range(3):
            at = base - DEPTH + tap * DEPTH
            shifted[tap, j] = pad[:, at : at + width, :].astype(BF)

    pixels = group * height * width
    wide = jnp.concatenate(
        [
            shifted[tap % 3, :, (tap // 3) * DEPTH : (tap // 3) * DEPTH + height].reshape(pixels, 128)
            for tap in range(9)
        ],
        axis=1,
    )
    pre = dot(wide, wc[...])
    half = 0.5 * (1.0 + lax.erf(pre * 0.7071067811865476))
    hidden = (pre * half).astype(BF)
    slope = half + pre * jnp.exp(-0.5 * pre * pre) * 0.3989422804014327

    part = dot(hidden, pj[...])
    part = part + jnp.where(col == 0, feat[...].reshape(pixels, 128).astype(F32), 0.0)
    quarter = pixels // 4
    blocks = (group * height // 2, width // 2, 128)
    resid_scr[...] = part.reshape(resid_scr.shape)
    grouped = jnp.concatenate(
        [
            resid_scr[:, ro, pl.ds(co, width // 2, stride=2), :].reshape(quarter, 128)
            for ro in range(2)
            for co in range(2)
        ],
        axis=1,
    )
    high = grouped.astype(BF)
    low = (grouped - high.astype(F32)).astype(BF)
    out = dot(high, dw[...]) + dot(low, dw[...])
    out_ref[...] = out.reshape(out_ref.shape)
    upstream = cot[...].reshape(quarter, 128)
    gd_ref[...] += dot(high, upstream, ((0,), (0,)))
    back = dot(upstream, dw[...], ((1,), (1,))).astype(BF).astype(F32)
    for ro in range(2):
        for co in range(2):
            at = (2 * ro + co) * 128
            resid_scr[:, ro, pl.ds(co, width // 2, stride=2), :] = back[:, at : at + 128].reshape(blocks)
    gresid = resid_scr[...].reshape(pixels, 128).astype(BF)
    pg_ref[...] += dot(hidden, gresid, ((0,), (0,)))
    gpre = (dot(gresid, pj[...], ((1,), (1,))) * slope).astype(BF)
    gc_ref[...] += dot(wide, gpre, ((0,), (0,)))


def run_block(edge, corner, place, feat, up, down_rows, near, own, far, sides, cot, wc, pj, dw, last_row):
    faces, height, width, channels = feat.shape
    hid = wc.shape[1]
    group = 3 if width <= 64 else 1
    tall = height + 2 * DEPTH
    smem = pl.BlockSpec(memory_space=pltpu.SMEM)

    def per_face(shape):
        return pl.BlockSpec((group,) + shape[1:], lambda s: (s, 0, 0, 0))

    def whole(shape):
        return pl.BlockSpec(shape, lambda s: (0,) * len(shape))

    out_shapes = (
        (faces, height // 2, width // 2, channels),
        (wc.shape[0], hid),
        (hid, channels),
        (4 * channels, channels),
    )
    flops = 2 * faces * height * width * (2 * 9 * channels * hid + 3 * hid * channels)
    return pl.pallas_call(
        functools.partial(block_kernel, group, last_row),
        grid=(faces // group,),
        in_specs=[
            smem, smem, smem,
            per_face(feat.shape), per_face(up.shape), per_face(down_rows.shape),
            whole(near.shape), whole(own.shape), whole(far.shape), whole(sides.shape),
            per_face(cot.shape), whole(wc.shape), whole(pj.shape), whole(dw.shape),
        ],
        out_specs=(
            per_face(out_shapes[0]),
            whole(out_shapes[1]), whole(out_shapes[2]), whole(out_shapes[3]),
        ),
        out_shape=tuple(jax.ShapeDtypeStruct(s, F32) for s in out_shapes),
        scratch_shapes=[
            pltpu.VMEM((tall, width + 16, channels), F32),
            pltpu.VMEM((3, group, tall, width, channels), BF),
            pltpu.VMEM((group * height // 2, 2, width, channels), F32),
        ],
        compiler_params=pltpu.CompilerParams(
            dimension_semantics=("arbitrary",), vmem_limit_bytes=56 << 20
        ),
        cost_estimate=pl.CostEstimate(
            flops=flops, transcendentals=2 * faces * height * width * hid, bytes_accessed=12 << 20
        ),
    )(edge, corner, place, feat, up, down_rows, near, own, far, sides, cot, wc, pj, dw)


def on_device(features, cotangent, conv_weight, projection_weight, down_weight, edge_links, corner_links):
    faces, height, breadth, channels = features.shape
    rows = lax.axis_size("row")
    cols = lax.axis_size("col")
    row = lax.axis_index("row")
    col = lax.axis_index("col")
    last = rows - 1
    tall = height + 2 * DEPTH
    width = cols * breadth
    hid = conv_weight.shape[1]
    part_rows = projection_weight.shape[0]

    feat = gather_pair(features, "col", 2)
    cot = gather_pair(cotangent, "col", 2)
    small = gather_pair(jnp.concatenate([projection_weight, down_weight], axis=0), "col", 1)
    packed = jnp.concatenate([pack_cols(conv_weight), small], axis=0)

    right = jnp.stack([feat[:, :, width - 1 - k] for k in range(DEPTH)], axis=1)
    left = jnp.stack([feat[:, :, k] for k in range(DEPTH)], axis=1)
    edges = jnp.stack([right, left])
    mirror = [(i, last - i) for i in range(rows)]
    mirrored = lax.ppermute(edges, "row", mirror)

    forward = [(i, i + 1) for i in range(last)]
    backward = [(i + 1, i) for i in range(last)]

    def rows_of(value):
        return value.reshape(-1, channels)

    going_down = jnp.concatenate(
        [rows_of(feat[:, height - DEPTH :]), rows_of(mirrored[:, :, :, :DEPTH])]
    )
    going_up = jnp.concatenate(
        [rows_of(feat[:, :DEPTH]), rows_of(mirrored[:, :, :, height - DEPTH :])]
    )
    from_above = lax.ppermute(going_down, "row", forward)
    from_below = lax.ppermute(going_up, "row", backward)
    cut = faces * DEPTH * width
    up = from_above[:cut].reshape(faces, DEPTH, width, channels)
    below = from_below[:cut].reshape(faces, DEPTH, width, channels)
    small_shape = (2, faces, DEPTH, DEPTH, channels)
    mirrored_tall = jnp.concatenate(
        [from_below[cut:].reshape(small_shape), mirrored, from_above[cut:].reshape(small_shape)],
        axis=3,
    )

    def side_columns(lines):
        return jnp.stack(
            [
                jnp.stack([lines[:, :, lines.shape[2] - 1 - k] for k in range(DEPTH)], axis=1),
                jnp.stack([lines[:, :, k] for k in range(DEPTH)], axis=1),
            ]
        )

    edges_tall = jnp.concatenate([side_columns(up), edges, side_columns(below)], axis=3)

    own = jnp.where(row == 0, feat[:, :DEPTH], feat[:, ::-1][:, :DEPTH])
    far = lax.ppermute(own, "row", [(0, last), (last, 0)])

    long = jnp.pad(own, ((0, 0), (0, 0), (DEPTH, DEPTH), (0, 0)))
    pieces = jnp.stack([rows_of(long[:, :, height * d : height * d + tall]) for d in range(rows)])
    pieces = jnp.where(col % 2 == 1, pieces[::-1], pieces)

    sides_of = edge_links[:, 0::2, :].transpose(1, 0, 2).reshape(2 * faces, 3)
    wanted = jnp.where(sides_of[:, 1] % 2 == 1, sides_of[:, 1] // 2 * faces + sides_of[:, 0], -1)
    choose = (wanted[:, None] == jnp.arange(2 * faces)[None, :]).astype(BF)

    def give(columns):
        flat = columns.reshape(2 * faces, DEPTH * height * channels)
        return dot(choose, flat).astype(BF).reshape(2, faces * DEPTH * height, channels)

    given = give(edges)
    given_mirrored = give(mirrored)
    fill = jnp.zeros((2, pieces.shape[1] - given.shape[1], channels), BF)
    given_long = jnp.concatenate([given, fill], axis=1)
    middle = jnp.zeros((rows - 2,) + given_long.shape[1:], BF)
    columns_out = jnp.concatenate([given_long[:1], middle, given_long[1:]])
    bands_out = jnp.where((row == 0) | (row == last), pieces, columns_out)

    half_rows = packed.shape[0] // 2
    weights_out = jnp.tile(packed.reshape(2, half_rows, channels), (rows // 2, 1, 1))
    sent = jnp.concatenate([weights_out, bands_out], axis=1)
    got = lax.all_to_all(sent, "row", 0, 0)

    got_half = got[:, :half_rows]
    other_half = swap(got_half, "row", 1)
    even = row % 2 == 0
    full = jnp.concatenate(
        [jnp.where(even, got_half, other_half), jnp.where(even, other_half, got_half)], axis=1
    )
    conv_rows = packed.shape[0] - 2 * part_rows
    wc = unpack_cols(full[:, :conv_rows], hid).reshape(rows * conv_weight.shape[0], hid)
    pj_all = full[:, conv_rows : conv_rows + part_rows].reshape(rows * part_rows, channels)
    pj = lax.dynamic_slice_in_dim(pj_all, col * hid, hid, 0)
    dw = full[:, conv_rows + part_rows :].reshape(rows * part_rows, channels)

    ends = jnp.stack([got[0, half_rows:], got[last, half_rows:]])
    ends_other = swap(ends, "col", 1)
    even_col = col % 2 == 0
    ends_shape = (2, faces, DEPTH, tall, channels)
    ends_direct = jnp.where(even_col, ends, ends_other).reshape(ends_shape)
    ends_mirror = jnp.where(even_col, ends_other, ends).reshape(ends_shape)

    def strips(ends_part, columns):
        return jnp.stack([ends_part[0], columns[0], ends_part[1], columns[1]])

    near = jnp.stack(
        [strips(ends_direct, edges_tall), strips(ends_mirror, mirrored_tall)]
    ).astype(F32)

    span = given.shape[1]
    mine = jnp.where(row == 0, given[0], given[1])
    theirs = jnp.where(row == 0, given_mirrored[0], given_mirrored[1])
    first = jnp.where(row == 0, mine, theirs)
    final = jnp.where(row == 0, theirs, mine)
    sides = jnp.concatenate(
        [first[None], got[1:last, half_rows : half_rows + span], final[None]]
    )
    sides = sides.reshape(rows, faces, DEPTH, height, channels).transpose(1, 2, 0, 3, 4)
    sides = sides.reshape(faces, DEPTH, rows * height, channels)

    place = jnp.stack([row, col]).astype(jnp.int32)
    out_part, gc, pg, gd = run_block(
        edge_links.reshape(-1), corner_links.reshape(-1), place,
        feat, up, below, near, own, far, sides, cot, wc, pj, dw, last,
    )

    block_out = scatter_sum_pair(out_part, "col", 2).astype(BF)
    gc_out = pack_cols(gc.astype(BF).reshape(rows, conv_weight.shape[0], hid))
    pg_wide = jnp.zeros((rows, part_rows, channels), BF)
    pg_wide = lax.dynamic_update_slice_in_dim(
        pg_wide, pg.astype(BF).reshape(-1, part_rows, channels), col * (rows // cols), 0
    )
    gd_out = gd.astype(BF).reshape(rows, part_rows, channels)
    shares = lax.all_to_all(jnp.concatenate([gc_out, pg_wide, gd_out], axis=1), "row", 0, 0)
    total = jnp.sum(shares.astype(F32), axis=0)
    grad_conv = unpack_cols(total[:conv_rows], hid)
    smaller = scatter_sum_pair(total[conv_rows:], "col", 1)
    return block_out, grad_conv, smaller[:part_rows], smaller[part_rows:]


def solution(mesh):
    return jax.shard_map(
        on_device,
        mesh=mesh,
        in_specs=(
            P(None, "row", "col", None),
            P(None, "row", "col", None),
            P("row", "col"),
            P("row", "col"),
            P("row", "col"),
            P(),
            P(),
        ),
        out_specs=(P(None, "row", "col", None), P("row", "col"), P("row", "col"), P("row", "col")),
        check_vma=False,
    )
```

```python
import functools

import jax
import jax.numpy as jnp
from jax import lax
from jax.experimental import pallas as pl
from jax.experimental.pallas import tpu as pltpu
from jax.sharding import PartitionSpec as P

DEPTH = 2
BF = jnp.bfloat16
F32 = jnp.float32


def swap(value, axis, bit):
    count = lax.axis_size(axis)
    return lax.ppermute(value, axis, [(i, i ^ bit) for i in range(count)])


def gather_pair(value, axis, dim):
    if lax.axis_size(axis) != 2:
        return lax.all_gather(value, axis, axis=dim, tiled=True)
    other = swap(value, axis, 1)
    first = lax.axis_index(axis) == 0
    low = jnp.where(first, value, other)
    high = jnp.where(first, other, value)
    return jnp.concatenate([low, high], axis=dim)


def scatter_sum_pair(value, axis, dim):
    count = lax.axis_size(axis)
    if count != 2:
        return lax.psum_scatter(value, axis, scatter_dimension=dim, tiled=True)
    low, high = jnp.split(value, 2, axis=dim)
    first = lax.axis_index(axis) == 0
    return jnp.where(first, low, high) + swap(jnp.where(first, high, low), axis, 1)


def pack_cols(value):
    width = value.shape[-1]
    if width % 128 == 0:
        return jnp.concatenate(
            [value[..., j : j + 128] for j in range(0, width, 128)], axis=-2
        )
    return value.reshape(value.shape[:-2] + (-1, 128))


def unpack_cols(value, width):
    if width % 128 == 0:
        parts = width // 128
        rows = value.shape[-2] // parts
        return jnp.concatenate(
            [value[..., j * rows : (j + 1) * rows, :] for j in range(parts)], axis=-1
        )
    return value.reshape(value.shape[:-2] + (-1, width))


def dot(a, b, dims=((1,), (0,))):
    return lax.dot_general(a, b, (dims, ((), ())), preferred_element_type=F32)


def block_kernel(
    group, last_row, edge, corner, where_ref,
    feat, up, down_rows, near, own, far, sides, cot, wc, pj, dw,
    out_ref, gc_ref, pg_ref, gd_ref,
    pad, shifted, resid_scr,
):
    step = pl.program_id(0)
    row = where_ref[0]
    col = where_ref[1]
    height, width = feat.shape[1], feat.shape[2]
    tall = height + 2 * DEPTH
    base = 8

    @pl.when(step == 0)
    def _():
        gc_ref[...] = jnp.zeros_like(gc_ref)
        pg_ref[...] = jnp.zeros_like(pg_ref)
        gd_ref[...] = jnp.zeros_like(gd_ref)

    line = lax.broadcasted_iota(jnp.int32, (width, width), 0)
    across = lax.broadcasted_iota(jnp.int32, (width, width), 1)
    flip = (line + across == width - 1).astype(BF)

    for j in range(group):
        face = step * group + j
        pad[DEPTH : DEPTH + height, base : base + width, :] = feat[j].astype(F32)
        pad[:DEPTH, base : base + width, :] = up[j].astype(F32)
        pad[DEPTH + height :, base : base + width, :] = down_rows[j].astype(F32)

        def link(side, what):
            return edge[face * 12 + side * 3 + what]

        for side, column in ((3, lambda k: base - 1 - k), (1, lambda k: base + width + k)):
            g, t, rev = link(side, 0), link(side, 1), link(side, 2)
            for k in range(DEPTH):
                for i in range(tall):
                    pick = jnp.where(rev == 1, tall - 1 - i, i)
                    pad[i, column(k) : column(k) + 1, :] = near[rev, t, g, k, pl.ds(pick, 1), :]

        def frame(side, corners, line_of, mine):
            g, t, rev = link(side, 0), link(side, 1), link(side, 2)
            for k in range(DEPTH):
                picked = jnp.where(
                    t == mine, own[g, k].astype(F32),
                    jnp.where(t == 2 - mine, far[g, k].astype(F32), sides[face, k].astype(F32)),
                ).astype(BF)
                turned = dot(flip, picked)
                pad[line_of(k), base : base + width, :] = jnp.where(
                    rev == 1, turned, picked.astype(F32)
                )
            for e, column in corners:
                cg = corner[face * 12 + e * 3]
                ce = corner[face * 12 + e * 3 + 1]
                cw = corner[face * 12 + e * 3 + 2]
                upper = ce < 2
                t = jnp.where((ce == 0) | (ce == 3), 3, 1)
                away = jnp.where(upper == (mine == 0), 0, 1)
                for a in range(DEPTH):
                    for b in range(DEPTH):
                        u = jnp.where(cw == 1, b, a)
                        v = jnp.where(cw == 1, a, b)
                        i = jnp.where(upper, DEPTH + u, tall - 1 - DEPTH - u)
                        value = near[away, t, jnp.maximum(cg, 0), v, pl.ds(i, 1), :]
                        pad[line_of(a), column(b) : column(b) + 1, :] = jnp.where(
                            cg >= 0, value, jnp.zeros_like(value)
                        )

        @pl.when(row == 0)
        def _():
            frame(
                0,
                ((0, lambda b: base - 1 - b), (1, lambda b: base + width + b)),
                lambda k: DEPTH - 1 - k,
                0,
            )

        @pl.when(row == last_row)
        def _():
            frame(
                2,
                ((3, lambda b: base - 1 - b), (2, lambda b: base + width + b)),
                lambda k: DEPTH + height + k,
                2,
            )

        for tap in range(3):
            at = base - DEPTH + tap * DEPTH
            shifted[tap, j] = pad[:, at : at + width, :].astype(BF)

    pixels = group * height * width
    wide = jnp.concatenate(
        [
            shifted[tap % 3, :, (tap // 3) * DEPTH : (tap // 3) * DEPTH + height].reshape(pixels, 128)
            for tap in range(9)
        ],
        axis=1,
    )
    pre = dot(wide, wc[...])
    half = 0.5 * (1.0 + lax.erf(pre * 0.7071067811865476))
    hidden = (pre * half).astype(BF)
    slope = half + pre * jnp.exp(-0.5 * pre * pre) * 0.3989422804014327

    part = dot(hidden, pj[...])
    part = part + jnp.where(col == 0, feat[...].reshape(pixels, 128).astype(F32), 0.0)
    quarter = pixels // 4
    blocks = (group * height // 2, width // 2, 128)
    resid_scr[...] = part.reshape(resid_scr.shape)
    grouped = jnp.concatenate(
        [
            resid_scr[:, ro, pl.ds(co, width // 2, stride=2), :].reshape(quarter, 128)
            for ro in range(2)
            for co in range(2)
        ],
        axis=1,
    )
    high = grouped.astype(BF)
    low = (grouped - high.astype(F32)).astype(BF)
    out = dot(high, dw[...]) + dot(low, dw[...])
    out_ref[...] = out.reshape(out_ref.shape)
    upstream = cot[...].reshape(quarter, 128)
    gd_ref[...] += dot(high, upstream, ((0,), (0,)))
    back = dot(upstream, dw[...], ((1,), (1,))).astype(BF).astype(F32)
    for ro in range(2):
        for co in range(2):
            at = (2 * ro + co) * 128
            resid_scr[:, ro, pl.ds(co, width // 2, stride=2), :] = back[:, at : at + 128].reshape(blocks)
    gresid = resid_scr[...].reshape(pixels, 128).astype(BF)
    pg_ref[...] += dot(hidden, gresid, ((0,), (0,)))
    gpre = (dot(gresid, pj[...], ((1,), (1,))) * slope).astype(BF)
    gc_ref[...] += dot(wide, gpre, ((0,), (0,)))


def run_block(edge, corner, place, feat, up, down_rows, near, own, far, sides, cot, wc, pj, dw, last_row):
    faces, height, width, channels = feat.shape
    hid = wc.shape[1]
    group = 3 if width <= 64 else 1
    tall = height + 2 * DEPTH
    smem = pl.BlockSpec(memory_space=pltpu.SMEM)

    def per_face(shape):
        return pl.BlockSpec((group,) + shape[1:], lambda s: (s, 0, 0, 0))

    def whole(shape):
        return pl.BlockSpec(shape, lambda s: (0,) * len(shape))

    out_shapes = (
        (faces, height // 2, width // 2, channels),
        (wc.shape[0], hid),
        (hid, channels),
        (4 * channels, channels),
    )
    flops = 2 * faces * height * width * (2 * 9 * channels * hid + 3 * hid * channels)
    return pl.pallas_call(
        functools.partial(block_kernel, group, last_row),
        grid=(faces // group,),
        in_specs=[
            smem, smem, smem,
            per_face(feat.shape), per_face(up.shape), per_face(down_rows.shape),
            whole(near.shape), whole(own.shape), whole(far.shape), whole(sides.shape),
            per_face(cot.shape), whole(wc.shape), whole(pj.shape), whole(dw.shape),
        ],
        out_specs=(
            per_face(out_shapes[0]),
            whole(out_shapes[1]), whole(out_shapes[2]), whole(out_shapes[3]),
        ),
        out_shape=tuple(jax.ShapeDtypeStruct(s, F32) for s in out_shapes),
        scratch_shapes=[
            pltpu.VMEM((tall, width + 16, channels), F32),
            pltpu.VMEM((3, group, tall, width, channels), BF),
            pltpu.VMEM((group * height // 2, 2, width, channels), F32),
        ],
        compiler_params=pltpu.CompilerParams(
            dimension_semantics=("arbitrary",), vmem_limit_bytes=56 << 20
        ),
        cost_estimate=pl.CostEstimate(
            flops=flops, transcendentals=2 * faces * height * width * hid, bytes_accessed=12 << 20
        ),
    )(edge, corner, place, feat, up, down_rows, near, own, far, sides, cot, wc, pj, dw)


def on_device(features, cotangent, conv_weight, projection_weight, down_weight, edge_links, corner_links):
    faces, height, breadth, channels = features.shape
    rows = lax.axis_size("row")
    cols = lax.axis_size("col")
    row = lax.axis_index("row")
    col = lax.axis_index("col")
    last = rows - 1
    tall = height + 2 * DEPTH
    width = cols * breadth
    hid = conv_weight.shape[1]
    part_rows = projection_weight.shape[0]
    pairs = rows // 2
    pair = row // 2
    core = row % 2
    even = core == 0
    pair_height = 2 * height
    pair_tall = pair_height + 2 * DEPTH
    same_core = [list(range(c, rows, 2)) for c in range(2)]
    is_end = (row == 0) | (row == last)

    def rows_of(value):
        return value.reshape(-1, channels)

    def join_core(mine, other, dim):
        return jnp.concatenate(
            [jnp.where(even, mine, other), jnp.where(even, other, mine)], axis=dim
        )

    strip = jnp.where(row == 0, features[:, :DEPTH], features[:, ::-1][:, :DEPTH])
    if cols == 2:
        lefts = jnp.stack([features[:, :, k] for k in range(DEPTH)], axis=1)
        rights = jnp.stack([features[:, :, breadth - 1 - k] for k in range(DEPTH)], axis=1)
        mine = jnp.where(col == 0, lefts, rights)
        seam = jnp.where(col == 0, strip[:, :, breadth - DEPTH :], strip[:, :, :DEPTH])
        cut = faces * DEPTH * height
        got = swap(jnp.concatenate([rows_of(mine), rows_of(seam)]), "col", 1)
        other = got[:cut].reshape(mine.shape)
        edges = jnp.stack([jnp.where(col == 0, other, mine), jnp.where(col == 0, mine, other)])
        seam_got = got[cut:].reshape(seam.shape)
        none = jnp.zeros_like(seam_got)
        long = jnp.concatenate(
            [jnp.where(col == 0, none, seam_got), strip, jnp.where(col == 0, seam_got, none)], axis=2
        )
        windows = jnp.stack(
            [rows_of(long[:, :, pair_height * d : pair_height * d + pair_tall]) for d in range(pairs // 2)]
        )
        ahead = jnp.concatenate([windows, windows[::-1]])
        behind = jnp.concatenate([windows[::-1], windows])
        pieces = jnp.where(col == 0, ahead, behind)
        direct_here = col == pair // (pairs // 2)
    else:
        ends = lax.all_gather(
            jnp.concatenate([features[:, :, :DEPTH], features[:, :, breadth - DEPTH :]], axis=2), "col"
        )
        edges = jnp.stack(
            [
                jnp.stack([ends[cols - 1, :, :, 2 * DEPTH - 1 - k] for k in range(DEPTH)], axis=1),
                jnp.stack([ends[0, :, :, k] for k in range(DEPTH)], axis=1),
            ]
        )
        whole = lax.all_gather(strip, "col", axis=2, tiled=True)
        long = jnp.pad(whole, ((0, 0), (0, 0), (DEPTH, DEPTH), (0, 0)))
        windows = jnp.stack(
            [rows_of(long[:, :, pair_height * d : pair_height * d + pair_tall]) for d in range(pairs)]
        )
        pieces = jnp.where(col % 2 == 0, windows, windows[::-1])
        direct_here = col % 2 == 0

    pair_edges = join_core(edges, swap(edges, "row", 1), 3)
    sides_of = jnp.where(even, edge_links[:, 0], edge_links[:, 2])
    wanted = jnp.where(sides_of[:, 1] % 2 == 1, sides_of[:, 1] // 2 * faces + sides_of[:, 0], -1)
    choose = (wanted[:, None] == jnp.arange(2 * faces)[None, :]).astype(BF)
    given = dot(choose, pair_edges.reshape(2 * faces, DEPTH * pair_height * channels)).astype(BF)
    given = given.reshape(faces * DEPTH * pair_height, channels)
    fill = jnp.zeros((pieces.shape[1] - given.shape[0], channels), BF)
    given_all = jnp.broadcast_to(jnp.concatenate([given, fill]), pieces.shape)
    bands_out = jnp.where(is_end, pieces, given_all)

    small = jnp.concatenate([projection_weight, down_weight], axis=1)
    small = pack_cols(small) if small.shape[1] != channels else small
    packed = jnp.concatenate([pack_cols(conv_weight), small], axis=0)
    weight_rows = packed.shape[0]
    weights_out = jnp.broadcast_to(packed, (pairs,) + packed.shape)
    sent = jnp.concatenate([weights_out, bands_out], axis=1)
    got = lax.all_to_all(sent, "row", 0, 0, axis_index_groups=same_core)

    across_pairs = [(i, i + 1) for i in range(1, last, 2)] + [(i + 1, i) for i in range(1, last, 2)]
    rim = jnp.where(even, features[:, :DEPTH], features[:, height - DEPTH :])
    rim_got = lax.ppermute(rim, "row", across_pairs)
    both = gather_pair(jnp.concatenate([features, rim_got], axis=1), "col", 2)
    feat = both[:, :height]
    outer = both[:, height:]
    inner = swap(jnp.where(even, feat[:, height - DEPTH :], feat[:, :DEPTH]), "row", 1)
    up = jnp.where(even, outer, inner)
    below = jnp.where(even, inner, outer)
    cot = gather_pair(cotangent, "col", 2)
    own = jnp.where(row == 0, feat[:, :DEPTH], feat[:, ::-1][:, :DEPTH])
    far = lax.ppermute(own, "row", [(0, last), (last, 0)])

    mirrored = lax.ppermute(edges, "row", [(i, last - i) for i in range(rows)])
    head = mirrored[:, :, :, :DEPTH]
    foot = mirrored[:, :, :, height - DEPTH :]
    mirror_inner = swap(jnp.where(even, head, foot), "row", 1)
    mirror_outer = lax.ppermute(jnp.where(even, foot, head), "row", across_pairs)
    mirrored_tall = jnp.concatenate(
        [
            jnp.where(even, mirror_inner, mirror_outer),
            mirrored,
            jnp.where(even, mirror_outer, mirror_inner),
        ],
        axis=3,
    )

    def side_columns(lines):
        return jnp.stack(
            [
                jnp.stack([lines[:, :, width - 1 - k] for k in range(DEPTH)], axis=1),
                jnp.stack([lines[:, :, k] for k in range(DEPTH)], axis=1),
            ]
        )

    edges_tall = jnp.concatenate([side_columns(up), edges, side_columns(below)], axis=3)

    conv_got = got[:, : weight_rows - small.shape[0]]
    conv_all = join_core(conv_got[:, None], swap(conv_got, "row", 1)[:, None], 1)
    wc = unpack_cols(conv_all, hid).reshape(rows * conv_weight.shape[0], hid)

    small_got = got[:, weight_rows - small.shape[0] : weight_rows]
    end = jnp.where(even, got[0, weight_rows:], got[pairs - 1, weight_rows:])
    if cols == 2:
        crossed = swap(jnp.concatenate([rows_of(small_got), end]), "col", 1)
        small_other = crossed[: pairs * part_rows].reshape(small_got.shape)
        end_other = crossed[pairs * part_rows :]
        low = jnp.where(col == 0, small_got, small_other)
        high = jnp.where(col == 0, small_other, small_got)
        cut = channels // 2
        pj_half = jnp.concatenate([low[..., :cut], high[..., :cut]], axis=-1)
        dw_half = jnp.concatenate([low[..., cut:], high[..., cut:]], axis=-1)
    else:
        end_other = swap(end, "col", 1)
        part = small_got.reshape(pairs, part_rows, 2 * projection_weight.shape[1])
        part = lax.all_gather(part, "col")
        part = part.transpose(1, 2, 0, 3)
        cut = projection_weight.shape[1]
        pj_half = part[..., :cut].reshape(pairs, part_rows, channels)
        dw_half = part[..., cut:].reshape(pairs, part_rows, channels)
    end_direct = jnp.where(direct_here, end, end_other)
    end_mirror = jnp.where(direct_here, end_other, end)
    bundle = jnp.concatenate([rows_of(pj_half), rows_of(dw_half), end_direct, end_mirror])
    bundle_other = swap(bundle, "row", 1)
    edge_of = pairs * part_rows

    def both_cores(start):
        return join_core(
            bundle[start : start + edge_of].reshape(pairs, 1, part_rows, channels),
            bundle_other[start : start + edge_of].reshape(pairs, 1, part_rows, channels),
            1,
        ).reshape(rows * part_rows, channels)

    pj = lax.dynamic_slice_in_dim(both_cores(0), col * hid, hid, 0)
    dw = both_cores(edge_of)
    span = end.shape[0]

    def ends_of(start, offset):
        both_ends = join_core(
            bundle[start : start + span][None], bundle_other[start : start + span][None], 0
        ).reshape(2, faces, DEPTH, pair_tall, channels)
        return jnp.where(
            even, both_ends[:, :, :, offset : offset + tall],
            both_ends[:, :, :, height - offset : height - offset + tall],
        )

    ends_direct = ends_of(2 * edge_of, 0)
    ends_mirror = ends_of(2 * edge_of + span, height)

    def strips(ends_part, columns):
        return jnp.stack([ends_part[0], columns[0], ends_part[1], columns[1]])

    near = jnp.stack(
        [strips(ends_direct, edges_tall), strips(ends_mirror, mirrored_tall)]
    ).astype(F32)

    sides = got[:, weight_rows : weight_rows + given.shape[0]]
    here = jnp.arange(pairs)[:, None, None] == pair
    sides = jnp.where(here, given[None], sides)
    sides = sides.reshape(pairs, faces, DEPTH, pair_height, channels).transpose(1, 2, 0, 3, 4)
    sides = sides.reshape(faces, DEPTH, rows * height, channels)

    place = jnp.stack([row, col]).astype(jnp.int32)
    out_part, gc, pg, gd = run_block(
        edge_links.reshape(-1), corner_links.reshape(-1), place,
        feat, up, below, near, own, far, sides, cot, wc, pj, dw, last,
    )

    gc_parts = gc.reshape(pairs, 2, conv_weight.shape[0], hid)
    pg_wide = jnp.zeros((rows, part_rows, channels), F32)
    pg_wide = lax.dynamic_update_slice_in_dim(
        pg_wide, pg.reshape(-1, part_rows, channels), col * (rows // cols), 0
    )
    pg_parts = pg_wide.reshape(pairs, 2, part_rows, channels)
    gd_parts = gd.reshape(pairs, 2, part_rows, channels)

    def mine_of(value):
        return jnp.where(even, value[:, 0], value[:, 1])

    def theirs_of(value):
        return jnp.where(even, value[:, 1], value[:, 0])

    def join_parts(pick):
        return jnp.concatenate([pack_cols(pick(gc_parts)), pick(pg_parts), pick(gd_parts)], axis=1)

    summed = (join_parts(mine_of) + swap(join_parts(theirs_of), "row", 1)).astype(BF)
    shares = lax.all_to_all(summed, "row", 0, 0, axis_index_groups=same_core)
    block_out = scatter_sum_pair(out_part, "col", 2).astype(BF)
    total = jnp.sum(shares.astype(F32), axis=0)
    conv_rows = total.shape[0] - 2 * part_rows
    grad_conv = unpack_cols(total[:conv_rows], hid)
    smaller = scatter_sum_pair(total[conv_rows:], "col", 1)
    return block_out, grad_conv, smaller[:part_rows], smaller[part_rows:]


def solution(mesh):
    return jax.shard_map(
        on_device,
        mesh=mesh,
        in_specs=(
            P(None, "row", "col", None),
            P(None, "row", "col", None),
            P("row", "col"),
            P("row", "col"),
            P("row", "col"),
            P(),
            P(),
        ),
        out_specs=(P(None, "row", "col", None), P("row", "col"), P("row", "col"), P("row", "col")),
        check_vma=False,
    )
```

```python
import functools

import jax
import jax.numpy as jnp
from jax import lax
from jax.experimental import pallas as pl
from jax.experimental.pallas import tpu as pltpu
from jax.sharding import PartitionSpec as P

DEPTH = 2
BF = jnp.bfloat16
F32 = jnp.float32


def swap(value, axis, bit):
    count = lax.axis_size(axis)
    return lax.ppermute(value, axis, [(i, i ^ bit) for i in range(count)])


def gather_pair(value, axis, dim):
    if lax.axis_size(axis) != 2:
        return lax.all_gather(value, axis, axis=dim, tiled=True)
    other = swap(value, axis, 1)
    first = lax.axis_index(axis) == 0
    low = jnp.where(first, value, other)
    high = jnp.where(first, other, value)
    return jnp.concatenate([low, high], axis=dim)


def scatter_sum_pair(value, axis, dim):
    count = lax.axis_size(axis)
    if count != 2:
        return lax.psum_scatter(value, axis, scatter_dimension=dim, tiled=True)
    low, high = jnp.split(value, 2, axis=dim)
    first = lax.axis_index(axis) == 0
    return jnp.where(first, low, high) + swap(jnp.where(first, high, low), axis, 1)


def pack_cols(value):
    width = value.shape[-1]
    if width % 128 == 0:
        return jnp.concatenate(
            [value[..., j : j + 128] for j in range(0, width, 128)], axis=-2
        )
    return value.reshape(value.shape[:-2] + (-1, 128))


def unpack_cols(value, width):
    if width % 128 == 0:
        parts = width // 128
        rows = value.shape[-2] // parts
        return jnp.concatenate(
            [value[..., j * rows : (j + 1) * rows, :] for j in range(parts)], axis=-1
        )
    return value.reshape(value.shape[:-2] + (-1, width))


def dot(a, b, dims=((1,), (0,))):
    return lax.dot_general(a, b, (dims, ((), ())), preferred_element_type=F32)


def block_kernel(
    group, last_row, edge, corner, where_ref,
    feat, up, down_rows, near, own, far, sides, cot, wc, pj_all, dw,
    out_ref, gc_ref, pg_ref, gd_ref,
    shifted, resid_scr,
):
    step = pl.program_id(0)
    row = where_ref[0]
    col = where_ref[1]
    height, width = feat.shape[1], feat.shape[2]
    tall = height + 2 * DEPTH
    hid = wc.shape[1]

    @pl.when(step == 0)
    def _():
        gc_ref[...] = jnp.zeros_like(gc_ref)
        pg_ref[...] = jnp.zeros_like(pg_ref)
        gd_ref[...] = jnp.zeros_like(gd_ref)

    def link(face, side, what):
        return edge[face * 12 + side * 3 + what]

    for j in range(group):
        face = step * group + j

        def column(side, k, i):
            g, t, rev = link(face, side, 0), link(face, side, 1), link(face, side, 2)
            return near[rev, t, g, k, pl.ds(jnp.where(rev == 1, tall - 1 - i, i), 1), :]

        for i in range(tall):
            if i < DEPTH:
                line = up[j, i]
            elif i < DEPTH + height:
                line = feat[j, i - DEPTH]
            else:
                line = down_rows[j, i - DEPTH - height]
            left = jnp.concatenate([column(3, k, i) for k in reversed(range(DEPTH))], axis=0)
            right = jnp.concatenate([column(1, k, i) for k in range(DEPTH)], axis=0)
            shifted[0, j, i] = jnp.concatenate([left.astype(BF), line[: width - DEPTH]], axis=0)
            shifted[1, j, i] = line
            shifted[2, j, i] = jnp.concatenate([line[DEPTH:], right.astype(BF)], axis=0)

    out_line = lax.broadcasted_iota(jnp.int32, (3 * width, width), 0)
    source = lax.broadcasted_iota(jnp.int32, (3 * width, width), 1)
    place = out_line % width + DEPTH * (out_line // width - 1)

    def frame(side, ends, line_of, mine):
        for j in range(group):
            face = step * group + j
            g, t, rev = link(face, side, 0), link(face, side, 1), link(face, side, 2)
            picked = jnp.concatenate(
                [
                    jnp.where(
                        t == mine, own[g, k].astype(F32),
                        jnp.where(t == 2 - mine, far[g, k].astype(F32), sides[face, k].astype(F32)),
                    ).astype(BF)
                    for k in range(DEPTH)
                ],
                axis=1,
            )
            move = (jnp.where(rev == 1, width - 1 - place, place) == source).astype(F32).astype(BF)
            turned = dot(move, picked).astype(BF)
            for k in range(DEPTH):
                for tap in range(3):
                    shifted[tap, j, line_of(k)] = turned[
                        tap * width : (tap + 1) * width, 128 * k : 128 * (k + 1)
                    ]
            for e, tap in zip(ends, (0, 2)):
                cg = corner[face * 12 + e * 3]
                ce = corner[face * 12 + e * 3 + 1]
                cw = corner[face * 12 + e * 3 + 2]
                upper = ce < 2
                side_of = jnp.where((ce == 0) | (ce == 3), 3, 1)
                away = jnp.where(upper == (mine == 0), 0, 1)

                def beyond(a, b):
                    u = jnp.where(cw == 1, b, a)
                    v = jnp.where(cw == 1, a, b)
                    i = jnp.where(upper, DEPTH + u, tall - 1 - DEPTH - u)
                    value = near[away, side_of, jnp.maximum(cg, 0), v, pl.ds(i, 1), :]
                    return jnp.where(cg >= 0, value, jnp.zeros_like(value))

                at = 0 if tap == 0 else width - DEPTH
                for a in range(DEPTH):
                    order = reversed(range(DEPTH)) if tap == 0 else range(DEPTH)
                    pixels_beyond = jnp.concatenate([beyond(a, b) for b in order], axis=0)
                    shifted[tap, j, line_of(a), at : at + DEPTH, :] = pixels_beyond.astype(BF)

    @pl.when(row == 0)
    def _():
        frame(0, (0, 1), lambda k: DEPTH - 1 - k, 0)

    @pl.when(row == last_row)
    def _():
        frame(2, (3, 2), lambda k: DEPTH + height + k, 2)

    pj = pj_all[pl.ds(pl.multiple_of(col * hid, hid), hid), :]
    pixels = group * height * width
    wide = jnp.concatenate(
        [
            shifted[tap % 3, :, (tap // 3) * DEPTH : (tap // 3) * DEPTH + height].reshape(pixels, 128)
            for tap in range(9)
        ],
        axis=1,
    )
    pre = dot(wide, wc[...])
    half = 0.5 * (1.0 + lax.erf(pre * 0.7071067811865476))
    hidden = (pre * half).astype(BF)
    slope = half + pre * jnp.exp(-0.5 * pre * pre) * 0.3989422804014327

    part = dot(hidden, pj)
    part = part + jnp.where(col == 0, feat[...].reshape(pixels, 128).astype(F32), 0.0)
    quarter = pixels // 4
    blocks = (group * height // 2, width // 2, 128)
    resid_scr[...] = part.reshape(resid_scr.shape)
    grouped = jnp.concatenate(
        [
            resid_scr[:, ro, pl.ds(co, width // 2, stride=2), :].reshape(quarter, 128)
            for ro in range(2)
            for co in range(2)
        ],
        axis=1,
    )
    high = grouped.astype(BF)
    low = (grouped - high.astype(F32)).astype(BF)
    out = dot(high, dw[...]) + dot(low, dw[...])
    out_ref[...] = out.reshape(out_ref.shape)
    upstream = cot[...].reshape(quarter, 128)
    gd_ref[...] += dot(high, upstream, ((0,), (0,)))
    back = dot(upstream, dw[...], ((1,), (1,))).astype(BF).astype(F32)
    for ro in range(2):
        for co in range(2):
            at = (2 * ro + co) * 128
            resid_scr[:, ro, pl.ds(co, width // 2, stride=2), :] = back[:, at : at + 128].reshape(blocks)
    gresid = resid_scr[...].reshape(pixels, 128).astype(BF)
    pg_ref[...] += dot(hidden, gresid, ((0,), (0,)))
    gpre = (dot(gresid, pj, ((1,), (1,))) * slope).astype(BF)
    gc_ref[...] += dot(wide, gpre, ((0,), (0,)))


def run_block(edge, corner, place, feat, up, down_rows, near, own, far, sides, cot, wc, pj, dw, last_row):
    faces, height, width, channels = feat.shape
    hid = wc.shape[1]
    group = 6 if width <= 64 else 1
    tall = height + 2 * DEPTH
    smem = pl.BlockSpec(memory_space=pltpu.SMEM)

    def per_face(shape):
        return pl.BlockSpec((group,) + shape[1:], lambda s: (s, 0, 0, 0))

    def whole(shape):
        return pl.BlockSpec(shape, lambda s: (0,) * len(shape))

    out_shapes = (
        (faces, height // 2, width // 2, channels),
        (wc.shape[0], hid),
        (hid, channels),
        (4 * channels, channels),
    )
    flops = 2 * faces * height * width * (2 * 9 * channels * hid + 3 * hid * channels)
    return pl.pallas_call(
        functools.partial(block_kernel, group, last_row),
        grid=(faces // group,),
        in_specs=[
            smem, smem, smem,
            per_face(feat.shape), per_face(up.shape), per_face(down_rows.shape),
            whole(near.shape), whole(own.shape), whole(far.shape), whole(sides.shape),
            per_face(cot.shape), whole(wc.shape), whole(pj.shape), whole(dw.shape),
        ],
        out_specs=(
            per_face(out_shapes[0]),
            whole(out_shapes[1]), whole(out_shapes[2]), whole(out_shapes[3]),
        ),
        out_shape=tuple(jax.ShapeDtypeStruct(s, F32) for s in out_shapes),
        scratch_shapes=[
            pltpu.VMEM((3, group, tall, width, channels), BF),
            pltpu.VMEM((group * height // 2, 2, width, channels), F32),
        ],
        compiler_params=pltpu.CompilerParams(
            dimension_semantics=("arbitrary",), vmem_limit_bytes=56 << 20
        ),
        cost_estimate=pl.CostEstimate(
            flops=flops, transcendentals=2 * faces * height * width * hid, bytes_accessed=12 << 20
        ),
    )(edge, corner, place, feat, up, down_rows, near, own, far, sides, cot, wc, pj, dw)


def on_device(features, cotangent, conv_weight, projection_weight, down_weight, edge_links, corner_links):
    faces, height, breadth, channels = features.shape
    rows = lax.axis_size("row")
    cols = lax.axis_size("col")
    row = lax.axis_index("row")
    col = lax.axis_index("col")
    last = rows - 1
    tall = height + 2 * DEPTH
    width = cols * breadth
    hid = conv_weight.shape[1]
    part_rows = projection_weight.shape[0]
    pairs = rows // 2
    pair = row // 2
    core = row % 2
    even = core == 0
    pair_height = 2 * height
    pair_tall = pair_height + 2 * DEPTH
    same_core = [list(range(c, rows, 2)) for c in range(2)]
    is_end = (row == 0) | (row == last)

    def rows_of(value):
        return value.reshape(-1, channels)

    def join_core(mine, other, dim):
        return jnp.concatenate(
            [jnp.where(even, mine, other), jnp.where(even, other, mine)], axis=dim
        )

    strip = jnp.where(row == 0, features[:, :DEPTH], features[:, ::-1][:, :DEPTH])
    if cols == 2:
        lefts = jnp.stack([features[:, :, k] for k in range(DEPTH)], axis=1)
        rights = jnp.stack([features[:, :, breadth - 1 - k] for k in range(DEPTH)], axis=1)
        mine = jnp.where(col == 0, lefts, rights)
        seam = jnp.where(col == 0, strip[:, :, breadth - DEPTH :], strip[:, :, :DEPTH])
        cut = faces * DEPTH * height
        got = swap(jnp.concatenate([rows_of(mine), rows_of(seam)]), "col", 1)
        other = got[:cut].reshape(mine.shape)
        edges = jnp.stack([jnp.where(col == 0, other, mine), jnp.where(col == 0, mine, other)])
        seam_got = got[cut:].reshape(seam.shape)
        none = jnp.zeros_like(seam_got)
        long = jnp.concatenate(
            [jnp.where(col == 0, none, seam_got), strip, jnp.where(col == 0, seam_got, none)], axis=2
        )
        windows = jnp.stack(
            [rows_of(long[:, :, pair_height * d : pair_height * d + pair_tall]) for d in range(pairs // 2)]
        )
        ahead = jnp.concatenate([windows, windows[::-1]])
        behind = jnp.concatenate([windows[::-1], windows])
        pieces = jnp.where(col == 0, ahead, behind)
        direct_here = col == pair // (pairs // 2)
    else:
        ends = lax.all_gather(
            jnp.concatenate([features[:, :, :DEPTH], features[:, :, breadth - DEPTH :]], axis=2), "col"
        )
        edges = jnp.stack(
            [
                jnp.stack([ends[cols - 1, :, :, 2 * DEPTH - 1 - k] for k in range(DEPTH)], axis=1),
                jnp.stack([ends[0, :, :, k] for k in range(DEPTH)], axis=1),
            ]
        )
        whole = lax.all_gather(strip, "col", axis=2, tiled=True)
        long = jnp.pad(whole, ((0, 0), (0, 0), (DEPTH, DEPTH), (0, 0)))
        windows = jnp.stack(
            [rows_of(long[:, :, pair_height * d : pair_height * d + pair_tall]) for d in range(pairs)]
        )
        pieces = jnp.where(col % 2 == 0, windows, windows[::-1])
        direct_here = col % 2 == 0

    pair_edges = join_core(edges, swap(edges, "row", 1), 3)
    sides_of = jnp.where(even, edge_links[:, 0], edge_links[:, 2])
    wanted = jnp.where(sides_of[:, 1] % 2 == 1, sides_of[:, 1] // 2 * faces + sides_of[:, 0], -1)
    choose = (wanted[:, None] == jnp.arange(2 * faces)[None, :]).astype(BF)
    given = dot(choose, pair_edges.reshape(2 * faces, DEPTH * pair_height * channels)).astype(BF)
    given = given.reshape(faces * DEPTH * pair_height, channels)
    fill = jnp.zeros((pieces.shape[1] - given.shape[0], channels), BF)
    given_all = jnp.broadcast_to(jnp.concatenate([given, fill]), pieces.shape)
    bands_out = jnp.where(is_end, pieces, given_all)

    small = jnp.concatenate([projection_weight, down_weight], axis=1)
    small = pack_cols(small) if small.shape[1] != channels else small
    packed = jnp.concatenate([pack_cols(conv_weight), small], axis=0)
    weight_rows = packed.shape[0]
    weights_out = jnp.broadcast_to(packed, (pairs,) + packed.shape)
    sent = jnp.concatenate([weights_out, bands_out], axis=1)
    sent, edge_table, corner_table, row_late = lax.optimization_barrier(
        (sent, edge_links, corner_links, row)
    )
    got = lax.all_to_all(sent, "row", 0, 0, axis_index_groups=same_core)

    across_pairs = [(i, i + 1) for i in range(1, last, 2)] + [(i + 1, i) for i in range(1, last, 2)]
    rim = jnp.where(even, features[:, :DEPTH], features[:, height - DEPTH :])
    rim_got = lax.ppermute(rim, "row", across_pairs)
    both = gather_pair(jnp.concatenate([features, rim_got], axis=1), "col", 2)
    feat = both[:, :height]
    outer = both[:, height:]
    inner = swap(jnp.where(even, feat[:, height - DEPTH :], feat[:, :DEPTH]), "row", 1)
    up = jnp.where(even, outer, inner)
    below = jnp.where(even, inner, outer)
    cot = gather_pair(cotangent, "col", 2)
    own = jnp.where(row == 0, feat[:, :DEPTH], feat[:, ::-1][:, :DEPTH])
    far = lax.ppermute(own, "row", [(0, last), (last, 0)])

    mirrored = lax.ppermute(edges, "row", [(i, last - i) for i in range(rows)])
    head = mirrored[:, :, :, :DEPTH]
    foot = mirrored[:, :, :, height - DEPTH :]
    mirror_inner = swap(jnp.where(even, head, foot), "row", 1)
    mirror_outer = lax.ppermute(jnp.where(even, foot, head), "row", across_pairs)
    mirrored_tall = jnp.concatenate(
        [
            jnp.where(even, mirror_inner, mirror_outer),
            mirrored,
            jnp.where(even, mirror_outer, mirror_inner),
        ],
        axis=3,
    )

    def side_columns(lines):
        return jnp.stack(
            [
                jnp.stack([lines[:, :, width - 1 - k] for k in range(DEPTH)], axis=1),
                jnp.stack([lines[:, :, k] for k in range(DEPTH)], axis=1),
            ]
        )

    edges_tall = jnp.concatenate([side_columns(up), edges, side_columns(below)], axis=3)

    conv_got = got[:, : weight_rows - small.shape[0]]
    conv_all = join_core(conv_got[:, None], swap(conv_got, "row", 1)[:, None], 1)
    wc = unpack_cols(conv_all, hid).reshape(rows * conv_weight.shape[0], hid)

    small_got = got[:, weight_rows - small.shape[0] : weight_rows]
    end = jnp.where(even, got[0, weight_rows:], got[pairs - 1, weight_rows:])
    if cols == 2:
        crossed = swap(jnp.concatenate([rows_of(small_got), end]), "col", 1)
        small_other = crossed[: pairs * part_rows].reshape(small_got.shape)
        end_other = crossed[pairs * part_rows :]
        low = jnp.where(col == 0, small_got, small_other)
        high = jnp.where(col == 0, small_other, small_got)
        cut = channels // 2
        pj_half = jnp.concatenate([low[..., :cut], high[..., :cut]], axis=-1)
        dw_half = jnp.concatenate([low[..., cut:], high[..., cut:]], axis=-1)
    else:
        end_other = swap(end, "col", 1)
        part = small_got.reshape(pairs, part_rows, 2 * projection_weight.shape[1])
        part = lax.all_gather(part, "col")
        part = part.transpose(1, 2, 0, 3)
        cut = projection_weight.shape[1]
        pj_half = part[..., :cut].reshape(pairs, part_rows, channels)
        dw_half = part[..., cut:].reshape(pairs, part_rows, channels)
    end_direct = jnp.where(direct_here, end, end_other)
    end_mirror = jnp.where(direct_here, end_other, end)
    bundle = jnp.concatenate([rows_of(pj_half), rows_of(dw_half), end_direct, end_mirror])
    bundle_other = swap(bundle, "row", 1)
    edge_of = pairs * part_rows

    def both_cores(start):
        return join_core(
            bundle[start : start + edge_of].reshape(pairs, 1, part_rows, channels),
            bundle_other[start : start + edge_of].reshape(pairs, 1, part_rows, channels),
            1,
        ).reshape(rows * part_rows, channels)

    pj = both_cores(0)
    dw = both_cores(edge_of)
    span = end.shape[0]

    def ends_of(start, offset):
        both_ends = join_core(
            bundle[start : start + span][None], bundle_other[start : start + span][None], 0
        ).reshape(2, faces, DEPTH, pair_tall, channels)
        return jnp.where(
            even, both_ends[:, :, :, offset : offset + tall],
            both_ends[:, :, :, height - offset : height - offset + tall],
        )

    ends_direct = ends_of(2 * edge_of, 0)
    ends_mirror = ends_of(2 * edge_of + span, height)

    def strips(ends_part, columns):
        return jnp.stack([ends_part[0], columns[0], ends_part[1], columns[1]])

    near = jnp.stack(
        [strips(ends_direct, edges_tall), strips(ends_mirror, mirrored_tall)]
    ).astype(F32)

    sides = got[:, weight_rows : weight_rows + given.shape[0]]
    here = jnp.arange(pairs)[:, None, None] == pair
    sides = jnp.where(here, given[None], sides)
    sides = sides.reshape(pairs, faces, DEPTH, pair_height, channels).transpose(1, 2, 0, 3, 4)
    sides = sides.reshape(faces, DEPTH, rows * height, channels)

    place = jnp.stack([row_late, col]).astype(jnp.int32)
    out_part, gc, pg, gd = run_block(
        edge_table.reshape(-1), corner_table.reshape(-1), place,
        feat, up, below, near, own, far, sides, cot, wc, pj, dw, last,
    )

    gc_parts = gc.reshape(pairs, 2, conv_weight.shape[0], hid)
    pg_wide = jnp.zeros((rows, part_rows, channels), F32)
    pg_wide = lax.dynamic_update_slice_in_dim(
        pg_wide, pg.reshape(-1, part_rows, channels), col * (rows // cols), 0
    )
    pg_parts = pg_wide.reshape(pairs, 2, part_rows, channels)
    gd_parts = gd.reshape(pairs, 2, part_rows, channels)

    def mine_of(value):
        return jnp.where(even, value[:, 0], value[:, 1])

    def theirs_of(value):
        return jnp.where(even, value[:, 1], value[:, 0])

    def join_parts(pick):
        return jnp.concatenate([pack_cols(pick(gc_parts)), pick(pg_parts), pick(gd_parts)], axis=1)

    summed = (join_parts(mine_of) + swap(join_parts(theirs_of), "row", 1)).astype(BF)
    shares = lax.all_to_all(summed, "row", 0, 0, axis_index_groups=same_core)
    block_out = scatter_sum_pair(out_part, "col", 2).astype(BF)
    total = jnp.sum(shares.astype(F32), axis=0)
    conv_rows = total.shape[0] - 2 * part_rows
    grad_conv = unpack_cols(total[:conv_rows], hid)
    smaller = scatter_sum_pair(total[conv_rows:], "col", 1)
    return block_out, grad_conv, smaller[:part_rows], smaller[part_rows:]


def solution(mesh):
    return jax.shard_map(
        on_device,
        mesh=mesh,
        in_specs=(
            P(None, "row", "col", None),
            P(None, "row", "col", None),
            P("row", "col"),
            P("row", "col"),
            P("row", "col"),
            P(),
            P(),
        ),
        out_specs=(P(None, "row", "col", None), P("row", "col"), P("row", "col"), P("row", "col")),
        check_vma=False,
    )
```

```python
import functools

import jax
import jax.numpy as jnp
from jax import lax
from jax.experimental import pallas as pl
from jax.experimental.pallas import tpu as pltpu
from jax.sharding import PartitionSpec as P

DEPTH = 2
BF = jnp.bfloat16
F32 = jnp.float32


def swap(value, axis, bit):
    count = lax.axis_size(axis)
    return lax.ppermute(value, axis, [(i, i ^ bit) for i in range(count)])


def gather_pair(value, axis, dim):
    if lax.axis_size(axis) != 2:
        return lax.all_gather(value, axis, axis=dim, tiled=True)
    other = swap(value, axis, 1)
    first = lax.axis_index(axis) == 0
    low = jnp.where(first, value, other)
    high = jnp.where(first, other, value)
    return jnp.concatenate([low, high], axis=dim)


def scatter_sum_pair(value, axis, dim):
    count = lax.axis_size(axis)
    if count != 2:
        return lax.psum_scatter(value, axis, scatter_dimension=dim, tiled=True)
    low, high = jnp.split(value, 2, axis=dim)
    first = lax.axis_index(axis) == 0
    return jnp.where(first, low, high) + swap(jnp.where(first, high, low), axis, 1)


def pack_cols(value):
    width = value.shape[-1]
    if width % 128 == 0:
        return jnp.concatenate(
            [value[..., j : j + 128] for j in range(0, width, 128)], axis=-2
        )
    return value.reshape(value.shape[:-2] + (-1, 128))


def unpack_cols(value, width):
    if width % 128 == 0:
        parts = width // 128
        rows = value.shape[-2] // parts
        return jnp.concatenate(
            [value[..., j * rows : (j + 1) * rows, :] for j in range(parts)], axis=-1
        )
    return value.reshape(value.shape[:-2] + (-1, width))


def dot(a, b, dims=((1,), (0,))):
    return lax.dot_general(a, b, (dims, ((), ())), preferred_element_type=F32)


def block_kernel(
    group, last_row, edge, corner, where_ref,
    feat, up, down_rows, near, own, far, sides, cot, wc, pj_all, dw,
    out_ref, gc_ref, pg_ref, gd_ref,
    shifted, resid_scr,
):
    step = pl.program_id(0)
    row = where_ref[0]
    col = where_ref[1]
    height, width = feat.shape[1], feat.shape[2]
    tall = height + 2 * DEPTH
    hid = wc.shape[1]

    @pl.when(step == 0)
    def _():
        gc_ref[...] = jnp.zeros_like(gc_ref)
        pg_ref[...] = jnp.zeros_like(pg_ref)
        gd_ref[...] = jnp.zeros_like(gd_ref)

    def link(face, side, what):
        return edge[face * 12 + side * 3 + what]

    for j in range(group):
        face = step * group + j

        def column(side, k, i):
            g, t, rev = link(face, side, 0), link(face, side, 1), link(face, side, 2)
            return near[rev, t, g, k, pl.ds(jnp.where(rev == 1, tall - 1 - i, i), 1), :]

        for i in range(tall):
            if i < DEPTH:
                line = up[j, i]
            elif i < DEPTH + height:
                line = feat[j, i - DEPTH]
            else:
                line = down_rows[j, i - DEPTH - height]
            left = jnp.concatenate([column(3, k, i) for k in reversed(range(DEPTH))], axis=0)
            right = jnp.concatenate([column(1, k, i) for k in range(DEPTH)], axis=0)
            shifted[0, j, i] = jnp.concatenate([left.astype(BF), line[: width - DEPTH]], axis=0)
            shifted[1, j, i] = line
            shifted[2, j, i] = jnp.concatenate([line[DEPTH:], right.astype(BF)], axis=0)

    out_line = lax.broadcasted_iota(jnp.int32, (3 * width, width), 0)
    source = lax.broadcasted_iota(jnp.int32, (3 * width, width), 1)
    place = out_line % width + DEPTH * (out_line // width - 1)

    def frame(side, ends, line_of, mine):
        for j in range(group):
            face = step * group + j
            g, t, rev = link(face, side, 0), link(face, side, 1), link(face, side, 2)
            picked = jnp.concatenate(
                [
                    jnp.where(
                        t == mine, own[g, k].astype(F32),
                        jnp.where(t == 2 - mine, far[g, k].astype(F32), sides[face, k].astype(F32)),
                    ).astype(BF)
                    for k in range(DEPTH)
                ],
                axis=1,
            )
            move = (jnp.where(rev == 1, width - 1 - place, place) == source).astype(F32).astype(BF)
            turned = dot(move, picked).astype(BF)
            for k in range(DEPTH):
                for tap in range(3):
                    shifted[tap, j, line_of(k)] = turned[
                        tap * width : (tap + 1) * width, 128 * k : 128 * (k + 1)
                    ]
            for e, tap in zip(ends, (0, 2)):
                cg = corner[face * 12 + e * 3]
                ce = corner[face * 12 + e * 3 + 1]
                cw = corner[face * 12 + e * 3 + 2]
                upper = ce < 2
                side_of = jnp.where((ce == 0) | (ce == 3), 3, 1)
                away = jnp.where(upper == (mine == 0), 0, 1)

                def beyond(a, b):
                    u = jnp.where(cw == 1, b, a)
                    v = jnp.where(cw == 1, a, b)
                    i = jnp.where(upper, DEPTH + u, tall - 1 - DEPTH - u)
                    value = near[away, side_of, jnp.maximum(cg, 0), v, pl.ds(i, 1), :]
                    return jnp.where(cg >= 0, value, jnp.zeros_like(value))

                at = 0 if tap == 0 else width - DEPTH
                for a in range(DEPTH):
                    order = reversed(range(DEPTH)) if tap == 0 else range(DEPTH)
                    pixels_beyond = jnp.concatenate([beyond(a, b) for b in order], axis=0)
                    shifted[tap, j, line_of(a), at : at + DEPTH, :] = pixels_beyond.astype(BF)

    @pl.when(row == 0)
    def _():
        frame(0, (0, 1), lambda k: DEPTH - 1 - k, 0)

    @pl.when(row == last_row)
    def _():
        frame(2, (3, 2), lambda k: DEPTH + height + k, 2)

    pj = pj_all[pl.ds(pl.multiple_of(col * hid, hid), hid), :]
    pixels = group * height * width
    wide = jnp.concatenate(
        [
            shifted[tap % 3, :, (tap // 3) * DEPTH : (tap // 3) * DEPTH + height].reshape(pixels, 128)
            for tap in range(9)
        ],
        axis=1,
    )
    pre = dot(wide, wc[...])
    half = 0.5 * (1.0 + lax.erf(pre * 0.7071067811865476))
    hidden = (pre * half).astype(BF)
    slope = half + pre * jnp.exp(-0.5 * pre * pre) * 0.3989422804014327

    part = dot(hidden, pj)
    part = part + jnp.where(col == 0, feat[...].reshape(pixels, 128).astype(F32), 0.0)
    quarter = pixels // 4
    blocks = (group * height // 2, width // 2, 128)
    resid_scr[...] = part.reshape(resid_scr.shape)
    grouped = jnp.concatenate(
        [
            resid_scr[:, ro, pl.ds(co, width // 2, stride=2), :].reshape(quarter, 128)
            for ro in range(2)
            for co in range(2)
        ],
        axis=1,
    )
    high = grouped.astype(BF)
    low = (grouped - high.astype(F32)).astype(BF)
    out = dot(high, dw[...]) + dot(low, dw[...])
    out_ref[...] = out.reshape(out_ref.shape)
    upstream = cot[...].reshape(quarter, 128)
    gd_ref[...] += dot(high, upstream, ((0,), (0,)))
    back = dot(upstream, dw[...], ((1,), (1,))).astype(BF).astype(F32)
    for ro in range(2):
        for co in range(2):
            at = (2 * ro + co) * 128
            resid_scr[:, ro, pl.ds(co, width // 2, stride=2), :] = back[:, at : at + 128].reshape(blocks)
    gresid = resid_scr[...].reshape(pixels, 128).astype(BF)
    pg_ref[...] += dot(hidden, gresid, ((0,), (0,)))
    gpre = (dot(gresid, pj, ((1,), (1,))) * slope).astype(BF)
    gc_ref[...] += dot(wide, gpre, ((0,), (0,)))


def run_block(edge, corner, place, feat, up, down_rows, near, own, far, sides, cot, wc, pj, dw, last_row):
    faces, height, width, channels = feat.shape
    hid = wc.shape[1]
    group = 6 if width <= 64 else 1
    tall = height + 2 * DEPTH
    smem = pl.BlockSpec(memory_space=pltpu.SMEM)

    def per_face(shape):
        return pl.BlockSpec((group,) + shape[1:], lambda s: (s, 0, 0, 0))

    def whole(shape):
        return pl.BlockSpec(shape, lambda s: (0,) * len(shape))

    out_shapes = (
        (faces, height // 2, width // 2, channels),
        (wc.shape[0], hid),
        (hid, channels),
        (4 * channels, channels),
    )
    flops = 2 * faces * height * width * (2 * 9 * channels * hid + 3 * hid * channels)
    return pl.pallas_call(
        functools.partial(block_kernel, group, last_row),
        grid=(faces // group,),
        in_specs=[
            smem, smem, smem,
            per_face(feat.shape), per_face(up.shape), per_face(down_rows.shape),
            whole(near.shape), whole(own.shape), whole(far.shape), whole(sides.shape),
            per_face(cot.shape), whole(wc.shape), whole(pj.shape), whole(dw.shape),
        ],
        out_specs=(
            per_face(out_shapes[0]),
            whole(out_shapes[1]), whole(out_shapes[2]), whole(out_shapes[3]),
        ),
        out_shape=tuple(jax.ShapeDtypeStruct(s, F32) for s in out_shapes),
        scratch_shapes=[
            pltpu.VMEM((3, group, tall, width, channels), BF),
            pltpu.VMEM((group * height // 2, 2, width, channels), F32),
        ],
        compiler_params=pltpu.CompilerParams(
            dimension_semantics=("arbitrary",), vmem_limit_bytes=56 << 20
        ),
        cost_estimate=pl.CostEstimate(
            flops=flops, transcendentals=2 * faces * height * width * hid, bytes_accessed=12 << 20
        ),
    )(edge, corner, place, feat, up, down_rows, near, own, far, sides, cot, wc, pj, dw)


def on_device(features, cotangent, conv_weight, projection_weight, down_weight, edge_links, corner_links):
    faces, height, breadth, channels = features.shape
    rows = lax.axis_size("row")
    cols = lax.axis_size("col")
    row = lax.axis_index("row")
    col = lax.axis_index("col")
    last = rows - 1
    tall = height + 2 * DEPTH
    width = cols * breadth
    hid = conv_weight.shape[1]
    part_rows = projection_weight.shape[0]
    pairs = rows // 2
    pair = row // 2
    core = row % 2
    even = core == 0
    pair_height = 2 * height
    pair_tall = pair_height + 2 * DEPTH
    same_core = [list(range(c, rows, 2)) for c in range(2)]
    is_end = (row == 0) | (row == last)

    def rows_of(value):
        return value.reshape(-1, channels)

    def join_core(mine, other, dim):
        return jnp.concatenate(
            [jnp.where(even, mine, other), jnp.where(even, other, mine)], axis=dim
        )

    strip = jnp.where(row == 0, features[:, :DEPTH], features[:, ::-1][:, :DEPTH])
    if cols == 2:
        lefts = jnp.stack([features[:, :, k] for k in range(DEPTH)], axis=1)
        rights = jnp.stack([features[:, :, breadth - 1 - k] for k in range(DEPTH)], axis=1)
        mine = jnp.where(col == 0, lefts, rights)
        seam = jnp.where(col == 0, strip[:, :, breadth - DEPTH :], strip[:, :, :DEPTH])
        cut = faces * DEPTH * height
        got = swap(jnp.concatenate([rows_of(mine), rows_of(seam)]), "col", 1)
        other = got[:cut].reshape(mine.shape)
        edges = jnp.stack([jnp.where(col == 0, other, mine), jnp.where(col == 0, mine, other)])
        seam_got = got[cut:].reshape(seam.shape)
        none = jnp.zeros_like(seam_got)
        long = jnp.concatenate(
            [jnp.where(col == 0, none, seam_got), strip, jnp.where(col == 0, seam_got, none)], axis=2
        )
        windows = jnp.stack(
            [rows_of(long[:, :, pair_height * d : pair_height * d + pair_tall]) for d in range(pairs // 2)]
        )
        ahead = jnp.concatenate([windows, windows[::-1]])
        behind = jnp.concatenate([windows[::-1], windows])
        pieces = jnp.where(col == 0, ahead, behind)
        direct_here = col == pair // (pairs // 2)
    else:
        ends = lax.all_gather(
            jnp.concatenate([features[:, :, :DEPTH], features[:, :, breadth - DEPTH :]], axis=2), "col"
        )
        edges = jnp.stack(
            [
                jnp.stack([ends[cols - 1, :, :, 2 * DEPTH - 1 - k] for k in range(DEPTH)], axis=1),
                jnp.stack([ends[0, :, :, k] for k in range(DEPTH)], axis=1),
            ]
        )
        whole = lax.all_gather(strip, "col", axis=2, tiled=True)
        long = jnp.pad(whole, ((0, 0), (0, 0), (DEPTH, DEPTH), (0, 0)))
        windows = jnp.stack(
            [rows_of(long[:, :, pair_height * d : pair_height * d + pair_tall]) for d in range(pairs)]
        )
        pieces = jnp.where(col % 2 == 0, windows, windows[::-1])
        direct_here = col % 2 == 0

    pair_edges = join_core(edges, swap(edges, "row", 1), 3)
    sides_of = jnp.where(even, edge_links[:, 0], edge_links[:, 2])
    wanted = jnp.where(sides_of[:, 1] % 2 == 1, sides_of[:, 1] // 2 * faces + sides_of[:, 0], -1)
    choose = (wanted[:, None] == jnp.arange(2 * faces)[None, :]).astype(BF)
    given = dot(choose, pair_edges.reshape(2 * faces, DEPTH * pair_height * channels)).astype(BF)
    given = given.reshape(faces * DEPTH * pair_height, channels)
    fill = jnp.zeros((pieces.shape[1] - given.shape[0], channels), BF)
    given_all = jnp.broadcast_to(jnp.concatenate([given, fill]), pieces.shape)
    bands_out = jnp.where(is_end, pieces, given_all)

    small = jnp.concatenate([projection_weight, down_weight], axis=1)
    small = pack_cols(small) if small.shape[1] != channels else small
    packed = jnp.concatenate([pack_cols(conv_weight), small], axis=0)
    weight_rows = packed.shape[0]
    weights_out = jnp.broadcast_to(packed, (pairs,) + packed.shape)
    sent = jnp.concatenate([weights_out, bands_out], axis=1)
    sent, edge_table, corner_table, row_late = lax.optimization_barrier(
        (sent, edge_links, corner_links, row)
    )
    got = lax.all_to_all(sent, "row", 0, 0, axis_index_groups=same_core)

    across_pairs = [(i, i + 1) for i in range(1, last, 2)] + [(i + 1, i) for i in range(1, last, 2)]
    rim = jnp.where(even, features[:, :DEPTH], features[:, height - DEPTH :])
    rim_got = lax.ppermute(rim, "row", across_pairs)
    both = gather_pair(jnp.concatenate([features, rim_got], axis=1), "col", 2)
    feat = both[:, :height]
    outer = both[:, height:]
    inner = swap(jnp.where(even, feat[:, height - DEPTH :], feat[:, :DEPTH]), "row", 1)
    up = jnp.where(even, outer, inner)
    below = jnp.where(even, inner, outer)
    cot = gather_pair(cotangent, "col", 2)
    own = jnp.where(row == 0, feat[:, :DEPTH], feat[:, ::-1][:, :DEPTH])
    far = lax.ppermute(own, "row", [(0, last), (last, 0)])

    mirrored = lax.ppermute(edges, "row", [(i, last - i) for i in range(rows)])
    head = mirrored[:, :, :, :DEPTH]
    foot = mirrored[:, :, :, height - DEPTH :]
    mirror_inner = swap(jnp.where(even, head, foot), "row", 1)
    mirror_outer = lax.ppermute(jnp.where(even, foot, head), "row", across_pairs)
    mirrored_tall = jnp.concatenate(
        [
            jnp.where(even, mirror_inner, mirror_outer),
            mirrored,
            jnp.where(even, mirror_outer, mirror_inner),
        ],
        axis=3,
    )

    def side_columns(lines):
        return jnp.stack(
            [
                jnp.stack([lines[:, :, width - 1 - k] for k in range(DEPTH)], axis=1),
                jnp.stack([lines[:, :, k] for k in range(DEPTH)], axis=1),
            ]
        )

    edges_tall = jnp.concatenate([side_columns(up), edges, side_columns(below)], axis=3)

    conv_got = got[:, : weight_rows - small.shape[0]]
    conv_all = join_core(conv_got[:, None], swap(conv_got, "row", 1)[:, None], 1)
    wc = unpack_cols(conv_all, hid).reshape(rows * conv_weight.shape[0], hid)

    small_got = got[:, weight_rows - small.shape[0] : weight_rows]
    end = jnp.where(even, got[0, weight_rows:], got[pairs - 1, weight_rows:])
    if cols == 2:
        crossed = swap(jnp.concatenate([rows_of(small_got), end]), "col", 1)
        small_other = crossed[: pairs * part_rows].reshape(small_got.shape)
        end_other = crossed[pairs * part_rows :]
        low = jnp.where(col == 0, small_got, small_other)
        high = jnp.where(col == 0, small_other, small_got)
        cut = channels // 2
        pj_half = jnp.concatenate([low[..., :cut], high[..., :cut]], axis=-1)
        dw_half = jnp.concatenate([low[..., cut:], high[..., cut:]], axis=-1)
    else:
        end_other = swap(end, "col", 1)
        part = small_got.reshape(pairs, part_rows, 2 * projection_weight.shape[1])
        part = lax.all_gather(part, "col")
        part = part.transpose(1, 2, 0, 3)
        cut = projection_weight.shape[1]
        pj_half = part[..., :cut].reshape(pairs, part_rows, channels)
        dw_half = part[..., cut:].reshape(pairs, part_rows, channels)
    end_direct = jnp.where(direct_here, end, end_other)
    end_mirror = jnp.where(direct_here, end_other, end)
    bundle = jnp.concatenate([rows_of(pj_half), rows_of(dw_half), end_direct, end_mirror])
    bundle_other = swap(bundle, "row", 1)
    edge_of = pairs * part_rows

    def both_cores(start):
        return join_core(
            bundle[start : start + edge_of].reshape(pairs, 1, part_rows, channels),
            bundle_other[start : start + edge_of].reshape(pairs, 1, part_rows, channels),
            1,
        ).reshape(rows * part_rows, channels)

    pj = both_cores(0)
    dw = both_cores(edge_of)
    span = end.shape[0]

    def ends_of(start, offset):
        both_ends = join_core(
            bundle[start : start + span][None], bundle_other[start : start + span][None], 0
        ).reshape(2, faces, DEPTH, pair_tall, channels)
        return jnp.where(
            even, both_ends[:, :, :, offset : offset + tall],
            both_ends[:, :, :, height - offset : height - offset + tall],
        )

    ends_direct = ends_of(2 * edge_of, 0)
    ends_mirror = ends_of(2 * edge_of + span, height)

    def strips(ends_part, columns):
        return jnp.stack([ends_part[0], columns[0], ends_part[1], columns[1]])

    near = jnp.stack(
        [strips(ends_direct, edges_tall), strips(ends_mirror, mirrored_tall)]
    ).astype(F32)

    sides = got[:, weight_rows : weight_rows + given.shape[0]]
    here = jnp.arange(pairs)[:, None, None] == pair
    sides = jnp.where(here, given[None], sides)
    sides = sides.reshape(pairs, faces, DEPTH, pair_height, channels).transpose(1, 2, 0, 3, 4)
    sides = sides.reshape(faces, DEPTH, rows * height, channels)

    place = jnp.stack([row_late, col]).astype(jnp.int32)
    out_part, gc, pg, gd = run_block(
        edge_table.reshape(-1), corner_table.reshape(-1), place,
        feat, up, below, near, own, far, sides, cot, wc, pj, dw, last,
    )

    gc_parts = gc.reshape(pairs, 2, conv_weight.shape[0], hid)
    pg_wide = jnp.zeros((rows * part_rows, channels), F32)
    pg_wide = lax.dynamic_update_slice_in_dim(pg_wide, pg, col * hid, 0)
    if cols == 2:
        cut = channels // 2
        low = jnp.concatenate([pg_wide[:, :cut], gd[:, :cut]], axis=1)
        high = jnp.concatenate([pg_wide[:, cut:], gd[:, cut:]], axis=1)
        joint = jnp.where(col == 0, low, high)
        joint = joint + swap(jnp.where(col == 0, high, low).astype(BF), "col", 1).astype(F32)
    else:
        joint = jnp.concatenate(
            [scatter_sum_pair(pg_wide, "col", 1), scatter_sum_pair(gd, "col", 1)], axis=1
        )
    joint_width = joint.shape[1]
    joint = joint.reshape(pairs, 2, part_rows, joint_width)

    def mine_of(value):
        return jnp.where(even, value[:, 0], value[:, 1])

    def theirs_of(value):
        return jnp.where(even, value[:, 1], value[:, 0])

    def narrow(value):
        return value if joint_width == channels else pack_cols(value)

    conv_sum = pack_cols(mine_of(gc_parts)) + swap(pack_cols(theirs_of(gc_parts)), "row", 1)
    joint_sum = narrow(mine_of(joint)) + swap(narrow(theirs_of(joint)), "row", 1)
    summed = jnp.concatenate([conv_sum, joint_sum], axis=1).astype(BF)
    shares = lax.all_to_all(summed, "row", 0, 0, axis_index_groups=same_core)
    block_out = scatter_sum_pair(out_part, "col", 2).astype(BF)
    total = jnp.sum(shares.astype(F32), axis=0)
    conv_rows = conv_sum.shape[1]
    grad_conv = unpack_cols(total[:conv_rows], hid)
    smaller = total[conv_rows:].reshape(part_rows, joint_width)
    cut = joint_width // 2
    return block_out, grad_conv, smaller[:, :cut], smaller[:, cut:]


def solution(mesh):
    return jax.shard_map(
        on_device,
        mesh=mesh,
        in_specs=(
            P(None, "row", "col", None),
            P(None, "row", "col", None),
            P("row", "col"),
            P("row", "col"),
            P("row", "col"),
            P(),
            P(),
        ),
        out_specs=(P(None, "row", "col", None), P("row", "col"), P("row", "col"), P("row", "col")),
        check_vma=False,
    )
```
